512 devices in a mesh: branch: 2 (over core), tm: 32 (over z_lo, y), tok: 8 (over z_hi, x).
Axes of the slice: x: 4, y: 4, z: 16 (z_hi: 2, z_lo: 8; z = z_hi * 8 + z_lo), core: 2. Of those that a mesh axis runs over, the one named last changes fastest.
Arguments:
- states: float32 [32, 512, 3072], P('tm', 'tok'), may hold values from -6 to 6
- start_state: float32 [512, 3072], P('tok', 'branch'), may hold values from -12 to 12
- timesteps: int32 [32], P('tm'), may hold values from 0 to 49
- guidance_index: int32 [1], replicated, may hold values from 0 to 7
- modulation: float32 [2, 3, 3072], P('branch'), may hold values from -2.5 to 2.5
- w_query: bfloat16 [3072, 2048], P('branch', 'tok'), may hold values from -6 to 6, as said below
- w_key: bfloat16 [3072, 2048], P('branch', 'tok'), may hold values from -6 to 6, as said below
- w_value: bfloat16 [3072, 2048], P('branch', 'tok'), may hold values from -0.109375 to 0.109375
- w_out: bfloat16 [2048, 3072], P('tok', 'branch'), may hold values from -0.5 to 0.5
Outputs:
- updated_states: float32 [32, 512, 3072], P('tm', 'tok', 'branch')
The draws below stay inside these ranges and needn't reach their ends.
Inputs may be any that keep to these rules, and one draw needn't show every extreme that they name: `w_query`: independent entries of mean zero. `w_key`: independent entries of mean zero.
All inputs are finite; a program needn't handle non-finite values.
Results may differ from the reference program's by a relative error of at most 0.0085.
The reference program's roundings to bfloat16 on the way count: a program that leaves them out, or rounds other values in their place, can miss the bound.
Values may be sent and summed in bfloat16 or wider, within the bound.
A program may use at most 64 MiB of HBM per device.

```python
import math
import jax
import jax.numpy as jnp
from jax import lax

D = 3072
HEADS = 16
HD = 128
NSTEPS = 50
LAT = 512
W = 32
N_TOK = 8


def projection_draw(seed_key):
    values = jnp.clip(jax.random.normal(seed_key, (D, HEADS * HD), jnp.float32), -6.0, 6.0) * D ** (-0.5)
    return values.astype(jnp.bfloat16)


def draw_w_query(key, part):
    return projection_draw(jax.random.fold_in(key, 11))


def draw_w_key(key, part):
    return projection_draw(jax.random.fold_in(key, 23))


def plant(values, rng, least, largest):
    shape = values.shape
    place = [jax.random.randint(jax.random.fold_in(rng, axis), (), 0, shape[axis]) for axis in range(len(shape))]
    values = values.at[tuple(place)].set(least)
    longest = shape.index(max(shape))
    place[longest] = (place[longest] + 1) % shape[longest]
    return values.at[tuple(place)].set(largest)


def steps_of(own_key, dims, cuts, least, largest):
    def one(axis_at, shards_of):
        draws = jax.random.uniform(jax.random.fold_in(jax.random.fold_in(own_key, 6), axis_at), (shards_of,), jnp.float32, least / len(cuts), largest / len(cuts))
        return jnp.repeat(jnp.exp(draws), dims[axis_at] // shards_of).reshape((-1,) + (1,) * (len(dims) - axis_at - 1))

    level = one(*cuts[0])
    for cut in cuts[1:]:
        level = level * one(*cut)
    return level


def centred(own_key, shape, deviation, bound, pieces=(), kind=jnp.bfloat16):
    array = jax.random.normal(own_key, shape, jnp.float32) * deviation
    if len(pieces) > 0:
        array = steps_of(own_key, shape, pieces, -0.22, 0.18) * array
    return jnp.clip(array, min=-bound, max=bound).astype(kind)


def setup_inputs(seed: int = 0) -> dict:
    seeds = jax.random.split(jax.random.key(seed), 10)
    return {
        "states": centred(seeds[0], (W, LAT, D), 1.0, 6.0, ((0, 32), (1, 8)), jnp.float32),
        "start_state": centred(seeds[1], (LAT, D), 2.0, 12.0, ((0, 8), (1, 2)), jnp.float32),
        "timesteps": plant(jax.random.randint(seeds[2], (W,), 0, NSTEPS), jax.random.fold_in(seeds[2], 1), 0, NSTEPS - 1).astype(jnp.int32),
        "guidance_index": jax.random.randint(seeds[3], (1,), 0, 8).astype(jnp.int32),
        "modulation": centred(seeds[4], (2, 3, D), 0.5, 2.5, ((0, 2),), jnp.float32),
        "w_query": draw_w_query(jax.random.fold_in(seeds[9], 71), 0),
        "w_key": draw_w_key(jax.random.fold_in(seeds[9], 71), 0),
        "w_value": centred(seeds[7], (D, HEADS * HD), D ** -0.5, 0.109375, ((0, 2), (1, 8))),
        "w_out": centred(seeds[8], (HEADS * HD, D), (HEADS * HD // 16) ** -0.5, 0.5, ((0, 8), (1, 2))),
    }


def embed(step_ids, model_width):
    half_width = model_width // 2
    frequency = jnp.exp(-math.log(10000.0) * jnp.arange(half_width, dtype=jnp.float32) / half_width)
    phases = step_ids.astype(jnp.float32)[:, None] * frequency[None, :]
    return jnp.concatenate([jnp.sin(phases), jnp.cos(phases)], axis=1)

def branch_drift(state_now, embedding, modulation_row, w_query, w_key, w_value, w_out):
    mean_value = lax.optimization_barrier(jnp.mean(state_now, axis=1, keepdims=True))
    centered = state_now - mean_value
    variance = lax.optimization_barrier(jnp.mean(centered * centered, axis=1, keepdims=True))
    normed = centered / jnp.sqrt(variance + 1e-06)
    modulated = (normed * (1.0 + modulation_row[1]) + modulation_row[0] + embedding).astype(jnp.bfloat16)
    query_proj = jnp.dot(modulated, w_query, preferred_element_type=jnp.float32).astype(jnp.bfloat16)
    key_proj = jnp.dot(modulated, w_key, preferred_element_type=jnp.float32).astype(jnp.bfloat16)
    value_proj = jnp.dot(modulated, w_value, preferred_element_type=jnp.float32).astype(jnp.bfloat16)
    query_heads = query_proj.reshape(LAT, HEADS, HD).astype(jnp.float32)
    key_heads = key_proj.reshape(LAT, HEADS, HD).astype(jnp.float32)
    value_heads = value_proj.reshape(LAT, HEADS, HD).astype(jnp.float32)
    scores = jnp.einsum('qhc,khc->hqk', query_heads, key_heads) * (1.0 / math.sqrt(HD))
    softmax_w = jax.nn.softmax(scores, axis=-1).astype(jnp.bfloat16)
    attended = jnp.einsum('hqk,khc->qhc', softmax_w.astype(jnp.float32), value_heads).astype(jnp.bfloat16)
    group_cols = HEADS * HD // N_TOK
    groups = attended.reshape(LAT, N_TOK, group_cols).astype(jnp.float32)
    out_groups = w_out.reshape(N_TOK, group_cols, D).astype(jnp.float32)
    partial_value = jnp.einsum('lgc,gcd->gld', groups, out_groups).astype(jnp.bfloat16)
    partial_value = lax.optimization_barrier(partial_value).astype(jnp.float32)
    projected = lax.optimization_barrier(jnp.sum(partial_value, axis=0))
    return (1.0 + modulation_row[2]) * projected

def reference(states, start_state, timesteps, guidance_index, modulation, w_query, w_key, w_value, w_out):
    guide_scale = 1.5 + 0.5 * guidance_index[0].astype(jnp.float32)

    def per_point(pair):
        state_now, step_id = pair
        embedding = embed(step_id[None], D)[0]
        conditional = branch_drift(state_now, embedding, modulation[0], w_query, w_key, w_value, w_out)
        unconditional = branch_drift(state_now, embedding, modulation[1], w_query, w_key, w_value, w_out)
        return unconditional + guide_scale * (conditional - unconditional)
    guided = lax.map(per_point, (states, timesteps))
    step_size = 2.0 * (1.0 + timesteps.astype(jnp.float32)) / NSTEPS
    increment = step_size[:, None, None] * guided
    return start_state[None, :, :] + jnp.cumsum(increment, axis=0)
```

```python
import functools
import math

import jax
import jax.numpy as jnp
from jax import lax
from jax.experimental import pallas as pl
from jax.experimental.pallas import tpu as pltpu
from jax.sharding import Mesh
from jax.sharding import PartitionSpec as P

HD = 128
NSTEPS = 50
BF = jnp.bfloat16
F32 = jnp.float32
AXES = ("b", "l", "y", "h", "x")


def embed(step_ids, model_width):
    half_width = model_width // 2
    frequency = jnp.exp(-math.log(10000.0) * jnp.arange(half_width, dtype=F32) / half_width)
    phases = step_ids.astype(F32)[:, None] * frequency[None, :]
    return jnp.concatenate([jnp.sin(phases), jnp.cos(phases)], axis=1)


def remote(src, dst, send_sem, recv_sem, device):
    return pltpu.make_async_remote_copy(
        src_ref=src,
        dst_ref=dst,
        send_sem=send_sem,
        recv_sem=recv_sem,
        device_id=device,
        device_id_type=pl.DeviceIdType.MESH,
    )


def kernel(
    nl, ny, nx, index,
    states, start, mod, emb, misc, w_query, w_key, w_value, w_out, out,
    xs, gathered, wq, qkv, att, relay, full, wo, acc, pre, ob, st, eb, sb, mp, ms, loc, ss, rs,
):
    b, l, y, h, x = (lax.axis_index(a) for a in AXES)
    rows, width = xs.shape
    half = width // 2
    quarter = half // ny
    cols = w_out.shape[0]
    head_count = cols // HD
    side_rows = nx * rows
    me = h * nx + x
    far = 1 - h
    other = far * nx + x
    opposite = {"h": far}
    partner = {"b": 1 - b}
    xto = [{"x": lax.rem(x + d, nx)} for d in range(nx)]
    xfrom = [lax.rem(x + nx - d, nx) for d in range(nx)]
    yto = [{"y": lax.rem(y + d, ny)} for d in range(ny)]
    yfrom = [lax.rem(y + ny - d, ny) for d in range(ny)]
    up = {"l": lax.rem(l + 1, nl), "h": jnp.where(l == nl - 1, far, h)}
    down = {"l": lax.rem(l + nl - 1, nl), "h": jnp.where(l == 0, far, h)}
    sent = []

    def sem(name):
        return index.setdefault(name, len(index))

    def send(name, src, dst, device):
        copy = remote(src, dst, ss.at[sem(name)], rs.at[sem(name)], device)
        copy.start()
        sent.append(copy)

    def arrived(name, dst):
        remote(dst, dst, ss.at[sem(name)], rs.at[sem(name)], partner).wait_recv()

    own_rows = pl.ds(pl.multiple_of(b * half, half), half)
    their_rows = pl.ds(pl.multiple_of((1 - b) * half, half), half)
    own_cols = pl.ds(pl.multiple_of(y * quarter, quarter), quarter)

    load = pltpu.make_async_copy(states.at[0], xs, loc.at[0])
    load.start()
    barrier = pltpu.get_barrier_semaphore()
    peers = [opposite, partner, up, down] + xto[1:] + yto[1:]
    for peer in peers:
        pl.semaphore_signal(barrier, inc=1, device_id=peer, device_id_type=pl.DeviceIdType.MESH)
    local = []
    for j, w in enumerate((w_query, w_key, w_value)):
        local.append(pltpu.make_async_copy(w, wq.at[j, own_rows], loc.at[1 + j]))
    local.append(pltpu.make_async_copy(start.at[:, own_cols], st, loc.at[4]))
    local.append(pltpu.make_async_copy(w_out.at[:, own_cols], wo.at[me], loc.at[5]))
    for copy in local:
        copy.start()
    ms[y] = misc[...]
    load.wait()

    @pl.loop(0, rows // 16)
    def _(r):
        at = pl.ds(pl.multiple_of(r * 16, 16), 16)
        value = xs[at, :]
        centered = value - jnp.mean(value, axis=1, keepdims=True)
        variance = jnp.mean(centered * centered, axis=1, keepdims=True)
        normed = centered / jnp.sqrt(variance + 1e-06)
        value = normed * (1.0 + mod[0, 1:2, :]) + mod[0, 0:1, :] + emb[...]
        gathered[me, at, :] = value.astype(BF)

    pl.semaphore_wait(barrier, len(peers))

    chunks = rows // 16
    for c in range(chunks):
        block = gathered.at[me, pl.ds(c * 16, 16)]
        send(("nz", c), block, block, opposite)
    for d in range(1, nx):
        send(("nx", d), gathered.at[me], gathered.at[me], xto[d])
    for j, w in enumerate((w_query, w_key, w_value)):
        send(("w", j), w, wq.at[j, own_rows], partner)
    send("mod", mod, mp, partner)
    for d in range(1, ny):
        send(("misc", d), misc, ms.at[y], yto[d])
    for copy in local:
        copy.wait()

    points = nl // 2
    distance = jnp.minimum(l, nl - 1 - l)
    inward = {"l": jnp.where(l < points, l + 1, l - 1)}
    edge = remote(
        wo.at[me], wo.at[me], ss.at[sem("edge")], rs.at[sem("chain")], {"l": nl - 1 - l, "h": far}
    )
    hop = remote(wo.at[other], wo.at[other], ss.at[sem("hop")], rs.at[sem("chain")], inward)
    pl.when(distance == 0)(edge.start)

    def chain_point(p):
        @pl.when(distance == p)
        def _():
            arrived("chain", wo.at[other])
            if p + 1 < points:
                hop.start()

    def project(side):
        to = pl.ds(pl.multiple_of(side * side_rows, side_rows), side_rows)

        @pl.loop(0, 3)
        def _(j):
            block = gathered[pl.ds(side * nx, nx)].reshape(side_rows, width)
            qkv[j, to, :] = jnp.dot(block, wq[j], preferred_element_type=F32).astype(BF)

    for j in range(3):
        arrived(("w", j), wq.at[j, their_rows])
    arrived("mod", mp)
    for d in range(1, nx):
        arrived(("nx", d), gathered.at[h * nx + xfrom[d]])

    def pass_on(c):
        block = gathered.at[other, pl.ds(c * 16, 16)]
        arrived(("nz", c), block)
        for d in range(1, nx):
            send(("nf", d, c), block, block, xto[d])

    pass_on(0)
    project(h)
    chain_point(0)
    for c in range(1, chunks):
        pass_on(c)
    for d in range(1, nx):
        send(("wx", d), wo.at[me], wo.at[me], xto[d])
    for p in range(1, points - 1):
        chain_point(p)
    for c in range(chunks):
        for d in range(1, nx):
            arrived(("nf", d, c), gathered.at[far * nx + xfrom[d], pl.ds(c * 16, 16)])
    project(far)

    def attend(side):
        to = pl.ds(pl.multiple_of(side * side_rows, side_rows), side_rows)
        for k in range(head_count):
            at = pl.ds(k * HD, HD)
            scores = lax.dot_general(
                qkv[0, to, at], qkv[1, :, at], (((1,), (1,)), ((), ())), preferred_element_type=F32
            ) * (1.0 / math.sqrt(HD))
            weight = jnp.exp(scores - jnp.max(scores, axis=1, keepdims=True))
            weight = weight / jnp.sum(weight, axis=1, keepdims=True)
            result = jnp.dot(weight.astype(BF), qkv[2, :, at], preferred_element_type=F32)
            att[pl.ds(side * nx, nx), :, at] = result.astype(BF).reshape(nx, rows, HD)

    order = list(range(1, nx)) + [0]
    attend(far)
    for d in order:
        send(("az", d), att.at[far * nx + lax.rem(x + d, nx)], relay.at[d], opposite)
    attend(h)
    for d in range(1, nx):
        send(("ax", 0, d), att.at[h * nx + lax.rem(x + d, nx)], full.at[me, y, b], xto[d])
    keep = pltpu.make_async_copy(att.at[me], full.at[me, y, b], loc.at[6])
    keep.start()
    keep.wait()

    def spread(side, part, d):
        block = full.at[side * nx + xfrom[d], y, b]
        if d:
            arrived(("ax", part, d), block)
        for e in range(1, ny):
            send(("ay", part, e, d), block, block, yto[e])

    def swap(side, part, e):
        blocks = full.at[pl.ds(side * nx, nx), yfrom[e], b]
        send(("ac", part, e), blocks, blocks, partner)

    def collect(side, part):
        for e in range(1, ny):
            for d in range(nx):
                arrived(("ay", part, e, d), full.at[side * nx + xfrom[d], yfrom[e], b])
            swap(side, part, e)

    def finish(side, part):
        for e in range(ny):
            arrived(("ac", part, e), full.at[pl.ds(side * nx, nx), yfrom[e], 1 - b])

    def multiply(side, first):
        for i in range(nx):
            group = side * nx + i
            block = full[group].reshape(ny * 2 * rows, cols)
            term = jnp.dot(block, wo[group], preferred_element_type=F32).astype(BF).astype(F32)
            if first and i == 0:
                acc[...] = term
            else:
                acc[...] += term

    for d in range(nx):
        spread(h, 0, d)
    swap(h, 0, 0)
    chain_point(points - 1)
    for d in range(1, nx):
        send(("wf", d), wo.at[other], wo.at[other], xto[d])
    collect(h, 0)

    for d in order:
        arrived(("az", d), relay.at[d])
        if d:
            send(("ax", 1, d), relay.at[d], full.at[other, y, b], xto[d])
        else:
            take = pltpu.make_async_copy(relay.at[0], full.at[other, y, b], loc.at[7])
            take.start()
            take.wait()
    for d in range(nx):
        spread(far, 1, d)
    swap(far, 1, 0)
    for d in range(1, nx):
        arrived(("wx", d), wo.at[h * nx + xfrom[d]])
    finish(h, 0)
    multiply(h, True)
    collect(far, 1)
    for d in range(1, nx):
        arrived(("wf", d), wo.at[far * nx + xfrom[d]])
    for e in range(1, ny):
        arrived(("misc", e), ms.at[yfrom[e]])
    finish(far, 1)
    multiply(far, False)

    channels = pl.ds(pl.multiple_of(b * half + y * quarter, quarter), quarter)
    own_gate = 1.0 + mod[0, 2:3, channels]
    their_gate = 1.0 + mp[0, 2:3, channels]
    gate_cond = jnp.where(b == 0, own_gate, their_gate)
    gate_free = jnp.where(b == 0, their_gate, own_gate)
    scale = misc[1:2, :]
    for i in range(ny):
        cond = gate_cond * acc[pl.ds(2 * i * rows, rows), :]
        free = gate_free * acc[pl.ds((2 * i + 1) * rows, rows), :]
        step = ms[i, 0:1, :] * (free + scale * (cond - free))
        pre[i] = step if i == 0 else pre[i - 1] + step

    @pl.when(l == 0)
    def _():
        eb[...] = jnp.zeros_like(eb)

    size = 16
    pieces = rows // size
    links = []
    for c in range(pieces):
        at = pl.ds(c * size, size)
        link = remote(
            sb.at[at], eb.at[at], ss.at[sem(("e", c))], rs.at[sem(("e", c))], {"l": lax.rem(l + 1, nl)}
        )
        links.append(link)

        @pl.when(l > 0)
        def _(at=at, c=c):
            arrived(("e", c), eb.at[at])

        @pl.when(l < nl - 1)
        def _(at=at, link=link):
            sb[at, :] = eb[at, :] + pre[ny - 1, at, :]
            link.start()

        base = st[at, :] + eb[at, :]
        for e in range(1, ny):
            ob[e, at, :] = base + pre[lax.rem(y + e, ny), at, :]
            send(("o", e, c), ob.at[e, at], out.at[0, at, own_cols], yto[e])
        out[0, at, own_cols] = base + pre[y, at, :]
    for c in range(pieces):
        for e in range(1, ny):
            columns = pl.ds(pl.multiple_of(yfrom[e] * quarter, quarter), quarter)
            arrived(("o", e, c), out.at[0, pl.ds(c * size, size), columns])

    for copy in sent:
        copy.wait_send()
    pl.when(distance == 0)(edge.wait_send)
    if points > 1:
        pl.when(distance < points - 1)(hop.wait_send)

    @pl.when(l < nl - 1)
    def _():
        for link in links:
            link.wait_send()


def body(nl, ny, nx, states, start, timesteps, guidance, modulation, w_query, w_key, w_value, w_out):
    _, rows, width = states.shape
    half = width // 2
    quarter = half // ny
    cols = w_out.shape[0]
    blocks = 2 * nx
    step = 2.0 * (1.0 + timesteps.astype(F32)) / NSTEPS
    scale = 1.5 + 0.5 * guidance.astype(F32)
    line = lax.broadcasted_iota(jnp.int32, (8, quarter), 0)
    misc = jnp.where(line == 0, step[0], scale[0])
    hbm = pl.BlockSpec(memory_space=pl.ANY)
    vmem = pl.BlockSpec(memory_space=pltpu.VMEM)
    return pl.pallas_call(
        functools.partial(kernel, nl, ny, nx, {}),
        out_shape=jax.ShapeDtypeStruct((1, rows, half), F32),
        in_specs=[hbm, hbm, vmem, vmem, vmem, hbm, hbm, hbm, hbm],
        out_specs=vmem,
        scratch_shapes=[
            pltpu.VMEM((rows, width), F32),
            pltpu.VMEM((blocks, rows, width), BF),
            pltpu.VMEM((3, width, cols), BF),
            pltpu.VMEM((3, blocks * rows, cols), BF),
            pltpu.VMEM((blocks, rows, cols), BF),
            pltpu.VMEM((nx, rows, cols), BF),
            pltpu.VMEM((blocks, ny, 2, rows, cols), BF),
            pltpu.VMEM((blocks, cols, quarter), BF),
            pltpu.VMEM((ny * 2 * rows, quarter), F32),
            pltpu.VMEM((ny, rows, quarter), F32),
            pltpu.VMEM((ny, rows, quarter), F32),
            pltpu.VMEM((rows, quarter), F32),
            pltpu.VMEM((rows, quarter), F32),
            pltpu.VMEM((rows, quarter), F32),
            pltpu.VMEM((1, 3, width), F32),
            pltpu.VMEM((ny, 8, quarter), F32),
            pltpu.SemaphoreType.DMA((8,)),
            pltpu.SemaphoreType.DMA((128,)),
            pltpu.SemaphoreType.DMA((128,)),
        ],
        compiler_params=pltpu.CompilerParams(
            collective_id=0, has_side_effects=True, vmem_limit_bytes=48 << 20
        ),
        name="picard",
    )(states, start, modulation, embed(timesteps, width), misc, w_query, w_key, w_value, w_out)


def build(fine, nl, ny, nx):
    tok = ("h", "x")
    tm = ("l", "y")
    placed = (
        P(tm, tok, None),
        P(tok, "b"),
        P(tm),
        P(),
        P("b", None, None),
        P("b", tok),
        P("b", tok),
        P("b", tok),
        P(tok, "b"),
    )
    return jax.shard_map(
        functools.partial(body, nl, ny, nx),
        mesh=fine,
        in_specs=placed,
        out_specs=P(tm, tok, "b"),
        check_vma=False,
    )


def solution(mesh):
    nl, ny, nx = 8, 4, 4
    return build(Mesh(mesh.devices.reshape(2, nl, ny, 2, nx), AXES), nl, ny, nx)
```
